32 devices in a mesh: groups: 2 (over y), replay: 4 (over z), module: 2 (over x), half: 2 (over core).
Axes of the slice: x: 2, y: 2, z: 4, core: 2. Of those that a mesh axis runs over, the one named last changes fastest.
Arguments:
- new_factors: bfloat16 [128, 2, 64, 128], P(('groups', 'replay', 'module')), parts along dimension 0, may hold values from -0.5 to 0.5
- new_counts: int32 [128], P(('groups', 'replay', 'module')), parts along dimension 0, may hold values from 32 to 64
- new_ids: int32 [128], P(('groups', 'module', 'half')), parts along dimension 0, may hold values from 0 to 3071
- replay_grads: bfloat16 [6144, 2, 4096], P(('groups', 'replay'), 'module', 'half'), parts along dimension 0, may hold values from -0.75 to 0.75
- replay_ids: int32 [6144], P(('groups', 'replay')), parts along dimension 0, may hold values from 0 to 3071
- slot_module: int32 [2], replicated, may hold values from 0 to 1, each once
- output_inverse: float32 [2, 64, 64], replicated, as said below
- input_inverse: float32 [2, 64, 64], replicated, as said below
Outputs:
- scores: float32 [128, 3072], P(('groups', 'module', 'half'), 'replay'), parts along dimension 0
The draws below stay inside these ranges and needn't reach their ends.
There are 2 independent parts, one for each index of `groups`. The reference program is written for one: setup_inputs(seed, part) draws one part's arguments, and reference() takes and returns one part's arrays. A program takes and returns all parts, laid end to end along the dimension named above; an argument that names none is the same for every part. Nothing has to cross between parts.
Inputs may be any that keep to these rules, and one draw needn't show every extreme that they name: `new_counts`: each new example has at least half of its token slots live, the live ones first. `slot_module`: each module sits in exactly one slot. `output_inverse`: symmetric with a positive diagonal. `input_inverse`: symmetric with a positive diagonal.
All inputs are finite; a program needn't handle non-finite values.
Results may differ from the reference program's by a relative error of at most 0.0029.
Values may be sent and summed in bfloat16 or wider, within the bound.
A program may use at most 64 MiB of HBM per device.

```python
import jax
import jax.numpy as jnp
from jax import lax

FEAT = 64
TOK = 64
MODULES = 2
NEW_TOTAL = 64
REPLAY_TOTAL = 3072


def inverse_factor(key, salt):
    seed_key = jax.random.fold_in(key, salt)
    diagonal_key, spread_key = jax.random.split(seed_key)
    eye_mask = jnp.eye(FEAT, dtype=jnp.float32)
    diagonal = jnp.exp(jax.random.uniform(diagonal_key, (MODULES, FEAT), jnp.float32, -0.7, 0.7))
    spread_part = 0.1 * jax.random.normal(spread_key, (MODULES, FEAT, FEAT), jnp.float32)
    symmetric = 0.7071 * (spread_part + jnp.swapaxes(spread_part, 1, 2))
    return symmetric * (1.0 - eye_mask) + diagonal[:, :, None] * eye_mask


def draw_output_inverse(key, part):
    return inverse_factor(key, 11)


def draw_input_inverse(key, part):
    return inverse_factor(key, 23)


def place_ends(result, key, low, top_value):
    extent = result.shape
    place = [jax.random.randint(jax.random.fold_in(key, axis), (), 0, extent[axis]) for axis in range(len(extent))]
    result = result.at[tuple(place)].set(low)
    longest = extent.index(max(extent))
    place[longest] = (place[longest] + 1) % extent[longest]
    return result.at[tuple(place)].set(top_value)


def block_scale(own_key, dims, pieces, least, high):
    def one(dim, blocks):
        steps = jax.random.uniform(jax.random.fold_in(jax.random.fold_in(own_key, 6), dim), (blocks,), jnp.float32, least / len(pieces), high / len(pieces))
        return jnp.repeat(jnp.exp(steps), dims[dim] // blocks).reshape((-1,) + (1,) * (len(dims) - dim - 1))

    loudness = one(*pieces[0])
    for cut in pieces[1:]:
        loudness = loudness * one(*cut)
    return loudness


def normal_values(stream_key, shape, spread, limit, shards=(), held_as=jnp.bfloat16):
    entries = jax.random.normal(stream_key, shape, jnp.float32) * spread
    if len(shards) > 0:
        entries = block_scale(stream_key, shape, shards, -0.22, 0.18) * entries
    return jnp.clip(entries, min=-limit, max=limit).astype(held_as)


def setup_inputs(seed: int = 0, part: int = 0) -> dict:
    splits = jax.random.split(jax.random.key(seed), 9)
    part_splits = jax.random.split(jax.random.fold_in(splits[8], part), 9)
    return {
        "new_factors": normal_values(part_splits[0], (NEW_TOTAL, MODULES, TOK, 2 * FEAT), 0.08, 0.5, ((0, 8),)),
        "new_counts": place_ends(jax.random.randint(part_splits[1], (NEW_TOTAL,), TOK // 2, TOK + 1), jax.random.fold_in(part_splits[1], 1), TOK // 2, TOK).astype(jnp.int32),
        "new_ids": place_ends(jax.random.randint(part_splits[2], (NEW_TOTAL,), 0, REPLAY_TOTAL), jax.random.fold_in(part_splits[2], 1), 0, REPLAY_TOTAL - 1).astype(jnp.int32),
        "replay_grads": normal_values(part_splits[3], (REPLAY_TOTAL, MODULES, FEAT * FEAT), 0.125, 0.75, ((0, 4), (1, 2), (2, 2))),
        "replay_ids": place_ends(jax.random.randint(part_splits[4], (REPLAY_TOTAL,), 0, REPLAY_TOTAL), jax.random.fold_in(part_splits[4], 1), 0, REPLAY_TOTAL - 1).astype(jnp.int32),
        "slot_module": jax.random.permutation(splits[5], MODULES).astype(jnp.int32),
        "output_inverse": draw_output_inverse(jax.random.fold_in(splits[8], 71), part),
        "input_inverse": draw_input_inverse(jax.random.fold_in(splits[8], 71), part),
    }


def reference(new_factors, new_counts, new_ids, replay_grads, replay_ids, slot_module, output_inverse, input_inverse):
    token_index = jnp.arange(TOK, dtype=jnp.int32)
    token_live = token_index[None, :] < new_counts[:, None]
    live_factors = jnp.where(token_live[:, None, :, None], new_factors, jnp.zeros((), jnp.bfloat16))
    raw = jnp.zeros((NEW_TOTAL, REPLAY_TOTAL), jnp.float32)
    for slot_index in range(MODULES):
        module_index = slot_module[slot_index]
        chosen = jnp.take(live_factors, module_index, axis=1)
        activations = chosen[:, :, :FEAT].astype(jnp.float32)
        output_grads = chosen[:, :, FEAT:].astype(jnp.float32)
        gradients = jnp.einsum('ntr,ntc->nrc', output_grads, activations)
        left_inverse = jnp.take(output_inverse, module_index, axis=0)
        right_inverse = jnp.take(input_inverse, module_index, axis=0)
        preconditioned = jnp.einsum('rk,nkc->nrc', left_inverse, gradients, precision=lax.Precision.HIGHEST)
        preconditioned = jnp.einsum('nrk,kc->nrc', preconditioned, right_inverse, precision=lax.Precision.HIGHEST)
        preconditioned = preconditioned.astype(jnp.bfloat16).reshape(NEW_TOTAL, FEAT * FEAT)
        raw = raw + lax.dot_general(preconditioned, replay_grads[:, slot_index, :], (((1,), (1,)), ((), ())), preferred_element_type=jnp.float32)
    self_pairs = new_ids[:, None] == replay_ids[None, :]
    return jnp.where(self_pairs, jnp.zeros((), jnp.float32), raw)
```

```python
import functools

import jax
import jax.numpy as jnp
from jax import lax
from jax.experimental import pallas as pl
from jax.experimental.pallas import tpu as pltpu
from jax.sharding import PartitionSpec as P

MESH = pl.DeviceIdType.MESH
UNROLL = 16


def each(count, step):
    if count <= UNROLL:
        for index in range(count):
            step(index)
    else:
        def one(index, carry):
            step(index)
            return carry

        lax.fori_loop(0, count, one, 0)


def parts_of(value):
    high = value.astype(jnp.bfloat16)
    low = (value - high.astype(jnp.float32)).astype(jnp.bfloat16)
    return high, low


def kernel(
    sizes,
    slot_module,
    counts,
    factors_hbm,
    replay_hbm,
    left_hbm,
    right_hbm,
    out_ref,
    factors,
    replay,
    left,
    right,
    rows_f32,
    outgoing,
    blocks,
    part,
    arrived,
    load_sem,
    send_sem,
    recv_sem,
    score_send_sem,
    score_recv_sem,
):
    replays, modules, halves, chunk = sizes
    z, x, h = lax.axis_index("replay"), lax.axis_index("module"), lax.axis_index("half")
    block = z * modules + x
    owner = x * halves + h
    owners = modules * halves
    examples, _, tokens, width = factors.shape
    feat = width // 2
    share = replay.shape[1] // feat
    columns = replay.shape[0]
    chunks = columns // chunk

    small_loads = [
        pltpu.make_async_copy(factors_hbm, factors, load_sem.at[0]),
        pltpu.make_async_copy(left_hbm, left, load_sem.at[1]),
        pltpu.make_async_copy(right_hbm, right, load_sem.at[2]),
    ]
    for load in small_loads:
        load.start()
    replay_load = pltpu.make_async_copy(replay_hbm, replay, load_sem.at[3])
    replay_load.start()

    barrier = pltpu.get_barrier_semaphore()

    def greet_block(offset):
        target = lax.rem(block + offset + 1, replays * modules)
        pl.semaphore_signal(
            barrier,
            inc=1,
            device_id={"replay": target // modules, "module": lax.rem(target, modules)},
            device_id_type=MESH,
        )

    def greet_owner(offset):
        index = lax.rem(h + offset % (halves - 1) + 1, halves)
        pl.semaphore_signal(
            barrier,
            inc=1,
            device_id={"module": offset // (halves - 1), "half": index},
            device_id_type=MESH,
        )

    each(replays * modules - 1, greet_block)
    for offset in range(modules * (halves - 1)):
        greet_owner(offset)

    for load in small_loads:
        load.wait()

    pair = 128 // tokens
    lane = lax.broadcasted_iota(jnp.int32, (share, 128), 1)
    zero = jnp.zeros((), jnp.bfloat16)
    low_lanes = lax.broadcasted_iota(jnp.int32, (examples, 2 * feat), 1) < feat

    def precondition(slot):
        module = slot_module[slot]
        entries = factors[:, module].reshape(examples * tokens, width)
        doubled = jnp.concatenate([entries, entries], axis=1)
        right_high, right_low = parts_of(right[module])
        blank = jnp.zeros((feat, feat), jnp.bfloat16)
        right_rows = jnp.concatenate([right_high, blank, right_low, blank], axis=0)
        right_rows = jnp.concatenate([right_rows, right_rows], axis=1)
        v = jnp.dot(doubled, right_rows, preferred_element_type=jnp.float32)
        left_high, left_low = parts_of(left[module, pl.ds(pl.multiple_of(h * share, share), share), :])
        left_blank = jnp.zeros((share, feat), jnp.bfloat16)
        left_columns = jnp.concatenate([left_blank, left_high, left_blank, left_low], axis=1)
        u = lax.dot_general(
            left_columns, doubled, (((1,), (1,)), ((), ())), preferred_element_type=jnp.float32
        )
        v_high, v_low = parts_of(v)
        for group in range(examples // pair):
            u_pair = u[:, group * 128 : (group + 1) * 128]
            masked = []
            for inner in range(pair):
                count = counts[group * pair + inner]
                first = inner * tokens
                keep = (lane >= first) & (lane < first + count)
                masked.append(jnp.where(keep, u_pair, 0.0))
            u_high, u_low = parts_of(jnp.concatenate(masked, axis=0))
            lhs = jnp.concatenate([u_high, u_high, u_low], axis=1)
            span = slice(group * 128, (group + 1) * 128)
            rhs = jnp.concatenate([v_high[span], v_low[span], v_high[span]], axis=0)
            rows_f32[pl.ds(group * pair * share, pair * share), :] = jnp.dot(
                lhs, rhs, preferred_element_type=jnp.float32
            )
        for q in range(share // 2):
            even = rows_f32[pl.ds(2 * q, examples, stride=share), :]
            odd = rows_f32[pl.ds(2 * q + 1, examples, stride=share), :]
            outgoing[slot, :, q * 2 * feat : (q + 1) * 2 * feat] = jnp.where(low_lanes, even, odd).astype(
                jnp.bfloat16
            )

    def block_copy(slot, target_z):
        target = target_z * modules + slot
        return pltpu.make_async_remote_copy(
            src_ref=outgoing.at[slot],
            dst_ref=blocks.at[block],
            send_sem=send_sem.at[target],
            recv_sem=recv_sem.at[block],
            device_id={"replay": target_z, "module": slot},
            device_id_type=MESH,
        )

    for step in range(modules):
        slot = lax.rem(x + 1 + step, modules)
        precondition(slot)
        if step == 0:
            pl.semaphore_wait(barrier, replays * modules - 1 + modules * (halves - 1))
        first = 0 if step < modules - 1 else 1
        each(replays - first, lambda index: block_copy(slot, lax.rem(z + first + index, replays)).start())
    blocks[block] = outgoing[x]

    def await_block(offset):
        source = lax.rem(block + offset + 1, replays * modules)
        pltpu.make_async_remote_copy(
            src_ref=outgoing.at[0],
            dst_ref=blocks.at[source],
            send_sem=send_sem.at[source],
            recv_sem=recv_sem.at[source],
            device_id={"replay": source // modules, "module": lax.rem(source, modules)},
            device_id_type=MESH,
        ).wait_recv()

    replay_load.wait()
    each(replays * modules - 1, await_block)

    total = replays * modules * examples
    rows = total // owners
    group_rows = min(total, 256)
    group_blocks = group_rows // examples

    def score_copy(target, c):
        cut = pl.ds(c * chunk, chunk)
        return pltpu.make_async_remote_copy(
            src_ref=part.at[pl.ds(pl.multiple_of(target * rows, rows), rows), cut],
            dst_ref=arrived.at[owner, :, cut],
            send_sem=score_send_sem.at[target, c],
            recv_sem=score_recv_sem.at[owner, c],
            device_id={"module": target // halves, "half": lax.rem(target, halves)},
            device_id_type=MESH,
        )

    def score_await(source, c):
        cut = pl.ds(c * chunk, chunk)
        return pltpu.make_async_remote_copy(
            src_ref=part.at[pl.ds(0, rows), cut],
            dst_ref=arrived.at[source, :, cut],
            send_sem=score_send_sem.at[source, c],
            recv_sem=score_recv_sem.at[source, c],
            device_id={"module": source // halves, "half": lax.rem(source, halves)},
            device_id_type=MESH,
        )

    for c in range(chunks):
        cut = slice(c * chunk, (c + 1) * chunk)

        def multiply(index):
            start = index * group_blocks
            lhs = blocks[pl.ds(start, group_blocks)].reshape(group_rows, blocks.shape[2])
            part[pl.ds(index * group_rows, group_rows), cut] = lax.dot_general(
                lhs, replay[cut, :], (((1,), (1,)), ((), ())), preferred_element_type=jnp.float32
            )

        if total == group_rows:
            multiply(0)
        else:
            pl.loop(0, total // group_rows)(multiply)
        for offset in range(1, owners):
            score_copy(lax.rem(owner + offset, owners), c).start()

    for c in range(chunks):
        cut = slice(c * chunk, (c + 1) * chunk)
        summed = part[pl.ds(pl.multiple_of(owner * rows, rows), rows), cut]
        for offset in range(1, owners):
            source = lax.rem(owner + offset, owners)
            score_await(source, c).wait_recv()
            summed = summed + arrived[source, :, cut]
        out_ref[:, cut] = summed

    def await_sent(offset):
        target = lax.rem(block + offset + 1, replays * modules)
        block_copy(lax.rem(target, modules), target // modules).wait_send()

    each(replays * modules - 1, await_sent)
    for c in range(chunks):
        for offset in range(1, owners):
            score_copy(lax.rem(owner + offset, owners), c).wait_send()


def body(
    replays,
    modules,
    halves,
    new_factors,
    new_counts,
    new_ids,
    replay_grads,
    replay_ids,
    slot_module,
    output_inverse,
    input_inverse,
):
    examples, _, _, width = new_factors.shape
    feat = width // 2
    columns, _, depth = replay_grads.shape
    share = depth // feat
    total = replays * modules * examples
    owners = modules * halves
    rows = total // owners
    chunk = 256 if columns % 256 == 0 else columns
    hbm = pl.BlockSpec(memory_space=pl.ANY)
    smem = pl.BlockSpec(memory_space=pltpu.SMEM)
    summed = pl.pallas_call(
        functools.partial(kernel, (replays, modules, halves, chunk)),
        out_shape=jax.ShapeDtypeStruct((rows, columns), jnp.float32),
        in_specs=[smem, smem, hbm, hbm, hbm, hbm],
        out_specs=pl.BlockSpec(memory_space=pltpu.VMEM),
        scratch_shapes=[
            pltpu.VMEM(new_factors.shape, jnp.bfloat16),
            pltpu.VMEM((columns, depth), jnp.bfloat16),
            pltpu.VMEM(output_inverse.shape, jnp.float32),
            pltpu.VMEM(input_inverse.shape, jnp.float32),
            pltpu.VMEM((examples * share, 2 * feat), jnp.float32),
            pltpu.VMEM((modules, examples, depth), jnp.bfloat16),
            pltpu.VMEM((replays * modules, examples, depth), jnp.bfloat16),
            pltpu.VMEM((total, columns), jnp.float32),
            pltpu.VMEM((owners, rows, columns), jnp.float32),
            pltpu.SemaphoreType.DMA((4,)),
            pltpu.SemaphoreType.DMA((replays * modules,)),
            pltpu.SemaphoreType.DMA((replays * modules,)),
            pltpu.SemaphoreType.DMA((owners, columns // chunk)),
            pltpu.SemaphoreType.DMA((owners, columns // chunk)),
        ],
        compiler_params=pltpu.CompilerParams(
            collective_id=0, has_side_effects=True, vmem_limit_bytes=60 * 1024 * 1024
        ),
        name="attribution",
    )(
        slot_module,
        new_counts,
        new_factors,
        replay_grads.reshape(columns, depth),
        output_inverse,
        input_inverse,
    )
    self_pairs = new_ids[:, None] == replay_ids[None, :]
    return jnp.where(self_pairs, jnp.zeros((), jnp.float32), summed)


def solution(mesh):
    in_specs = (
        P(("groups", "replay", "module"), None, None, None),
        P(("groups", "replay", "module")),
        P(("groups", "module", "half")),
        P(("groups", "replay"), "module", "half"),
        P(("groups", "replay")),
        P(),
        P(),
        P(),
    )
    out_specs = P(("groups", "module", "half"), "replay")
    return jax.shard_map(
        functools.partial(body, mesh.shape["replay"], mesh.shape["module"], mesh.shape["half"]),
        mesh=mesh,
        in_specs=in_specs,
        out_specs=out_specs,
        check_vma=False,
    )
```

```python
import functools

import jax
import jax.numpy as jnp
from jax import lax
from jax.experimental import pallas as pl
from jax.experimental.pallas import tpu as pltpu
from jax.sharding import PartitionSpec as P

MESH = pl.DeviceIdType.MESH
UNROLL = 16
EARLY = 1
LATE = 2


def each(count, step):
    if count <= UNROLL:
        for index in range(count):
            step(index)
    else:
        def one(index, carry):
            step(index)
            return carry

        lax.fori_loop(0, count, one, 0)


def parts_of(value):
    high = value.astype(jnp.bfloat16)
    low = (value - high.astype(jnp.float32)).astype(jnp.bfloat16)
    return high, low


def kernel(
    sizes,
    slot_module,
    counts,
    factors_hbm,
    replay_hbm,
    left_hbm,
    right_hbm,
    out_ref,
    factors,
    replay,
    left,
    right,
    rows_f32,
    outgoing,
    blocks,
    part,
    arrived,
    load_sem,
    send_sem,
    recv_sem,
    score_send_sem,
    score_recv_sem,
):
    replays, modules, halves, chunk = sizes
    z, x, h = lax.axis_index("replay"), lax.axis_index("module"), lax.axis_index("half")
    block = z * modules + x
    owner = x * halves + h
    owners = modules * halves
    examples, _, tokens, width = factors.shape
    feat = width // 2
    share = replay.shape[1] // feat
    columns = replay.shape[0]
    chunks = columns // chunk

    small_loads = [
        pltpu.make_async_copy(factors_hbm, factors, load_sem.at[0]),
        pltpu.make_async_copy(left_hbm, left, load_sem.at[1]),
        pltpu.make_async_copy(right_hbm, right, load_sem.at[2]),
    ]
    for load in small_loads:
        load.start()
    replay_load = pltpu.make_async_copy(replay_hbm, replay, load_sem.at[3])
    replay_load.start()

    barrier = pltpu.get_barrier_semaphore()

    def greet_block(offset):
        target = lax.rem(block + offset + 1, replays * modules)
        pl.semaphore_signal(
            barrier,
            inc=1,
            device_id={"replay": target // modules, "module": lax.rem(target, modules)},
            device_id_type=MESH,
        )

    def greet_owner(offset):
        index = lax.rem(h + offset % (halves - 1) + 1, halves)
        pl.semaphore_signal(
            barrier,
            inc=1,
            device_id={"module": offset // (halves - 1), "half": index},
            device_id_type=MESH,
        )

    each(replays * modules - 1, greet_block)
    for offset in range(modules * (halves - 1)):
        greet_owner(offset)

    for load in small_loads:
        load.wait()

    pair = 128 // tokens
    lane = lax.broadcasted_iota(jnp.int32, (share, 128), 1)
    zero = jnp.zeros((), jnp.bfloat16)
    low_lanes = lax.broadcasted_iota(jnp.int32, (examples, 2 * feat), 1) < feat

    def precondition(slot):
        module = slot_module[slot]
        entries = factors[:, module].reshape(examples * tokens, width)
        doubled = jnp.concatenate([entries, entries], axis=1)
        right_high, right_low = parts_of(right[module])
        blank = jnp.zeros((feat, feat), jnp.bfloat16)
        right_rows = jnp.concatenate([right_high, blank, right_low, blank], axis=0)
        right_rows = jnp.concatenate([right_rows, right_rows], axis=1)
        v = jnp.dot(doubled, right_rows, preferred_element_type=jnp.float32)
        left_high, left_low = parts_of(left[module, pl.ds(pl.multiple_of(h * share, share), share), :])
        left_blank = jnp.zeros((share, feat), jnp.bfloat16)
        left_columns = jnp.concatenate([left_blank, left_high, left_blank, left_low], axis=1)
        u = lax.dot_general(
            left_columns, doubled, (((1,), (1,)), ((), ())), preferred_element_type=jnp.float32
        )
        v_high, v_low = parts_of(v)
        for group in range(examples // pair):
            u_pair = u[:, group * 128 : (group + 1) * 128]
            masked = []
            for inner in range(pair):
                count = counts[group * pair + inner]
                first = inner * tokens
                keep = (lane >= first) & (lane < first + count)
                masked.append(jnp.where(keep, u_pair, 0.0))
            u_high, u_low = parts_of(jnp.concatenate(masked, axis=0))
            lhs = jnp.concatenate([u_high, u_high, u_low], axis=1)
            span = slice(group * 128, (group + 1) * 128)
            rhs = jnp.concatenate([v_high[span], v_low[span], v_high[span]], axis=0)
            rows_f32[pl.ds(group * pair * share, pair * share), :] = jnp.dot(
                lhs, rhs, preferred_element_type=jnp.float32
            )
        for q in range(share // 2):
            even = rows_f32[pl.ds(2 * q, examples, stride=share), :]
            odd = rows_f32[pl.ds(2 * q + 1, examples, stride=share), :]
            outgoing[slot, :, q * 2 * feat : (q + 1) * 2 * feat] = jnp.where(low_lanes, even, odd).astype(
                jnp.bfloat16
            )

    def block_copy(slot, target_z):
        target = target_z * modules + slot
        return pltpu.make_async_remote_copy(
            src_ref=outgoing.at[slot],
            dst_ref=blocks.at[block],
            send_sem=send_sem.at[target],
            recv_sem=recv_sem.at[block],
            device_id={"replay": target_z, "module": slot},
            device_id_type=MESH,
        )

    for slot in range(modules):
        precondition(slot)
    blocks[block] = outgoing[x]
    pl.semaphore_wait(barrier, replays * modules - 1 + modules * (halves - 1))

    def neighbour(step):
        if replays & (replays - 1):
            return lax.rem(z + step, replays)
        other, bit = z, 1
        while bit < replays:
            other = other + bit * ((step // bit) % 2) * (1 - 2 * ((z // bit) % 2))
            bit *= 2
        return other

    def send_blocks(step):
        for offset in range(1, modules):
            block_copy(lax.rem(x + offset, modules), neighbour(step)).start()
        if not (isinstance(step, int) and step == 0):
            block_copy(x, neighbour(step)).start()

    send_blocks(0)
    each(replays - 1, lambda index: send_blocks(1 + (index + 1) % (replays - 1)))

    per_owner = replays // owners
    step_rows = modules * examples

    def await_block(slot, source):
        pltpu.make_async_remote_copy(
            src_ref=outgoing.at[0],
            dst_ref=blocks.at[source],
            send_sem=send_sem.at[source],
            recv_sem=recv_sem.at[source],
            device_id={"replay": source // modules, "module": slot},
            device_id_type=MESH,
        ).wait_recv()

    def score_copy(source, c):
        cut = pl.ds(c * chunk, chunk)
        target = source // per_owner
        return pltpu.make_async_remote_copy(
            src_ref=part.at[pl.ds(pl.multiple_of(source * step_rows, step_rows), step_rows), cut],
            dst_ref=arrived.at[
                owner, pl.ds(pl.multiple_of((source % per_owner) * step_rows, step_rows), step_rows), cut
            ],
            send_sem=score_send_sem.at[source, c],
            recv_sem=score_recv_sem.at[owner, source % per_owner, c],
            device_id={"module": target // halves, "half": target % halves},
            device_id_type=MESH,
        )

    def score_await(source, inner, c):
        cut = pl.ds(c * chunk, chunk)
        return pltpu.make_async_remote_copy(
            src_ref=part.at[pl.ds(0, step_rows), cut],
            dst_ref=arrived.at[source, pl.ds(inner * step_rows, step_rows), cut],
            send_sem=score_send_sem.at[0, c],
            recv_sem=score_recv_sem.at[source, inner, c],
            device_id={"module": source // halves, "half": source % halves},
            device_id_type=MESH,
        )

    replay_load.wait()

    def await_step(step):
        source = neighbour(step)
        for offset in range(1, modules):
            slot = lax.rem(x + offset, modules)
            await_block(slot, source * modules + slot)
        if not (isinstance(step, int) and step == 0):
            await_block(x, source * modules + x)

    def score_steps(first, count, pieces):
        sources = [neighbour(first + inner) for inner in range(count)]
        lhs = jnp.concatenate(
            [blocks[source * modules + slot] for source in sources for slot in range(modules)], axis=0
        )
        for piece in range(pieces):
            span = columns // pieces
            cut = slice(piece * span, (piece + 1) * span)
            scores = lax.dot_general(
                lhs, replay[cut, :], (((1,), (1,)), ((), ())), preferred_element_type=jnp.float32
            )
            for inner, source in enumerate(sources):
                part[pl.ds(pl.multiple_of(source * step_rows, step_rows), step_rows), cut] = scores[
                    inner * step_rows : (inner + 1) * step_rows
                ]
            for source in sources:

                @pl.when(source // per_owner != owner)
                def _():
                    for c in range(piece * span // chunk, (piece + 1) * span // chunk):
                        score_copy(source, c).start()

    batch = 2 if replays % 2 == 0 else 1
    for inner in range(batch):
        await_step(inner)
    score_steps(0, batch, EARLY)

    def later(index):
        for inner in range(batch):
            await_step((index + 1) * batch + inner)
        score_steps((index + 1) * batch, batch, LATE)

    each(replays // batch - 1, later)

    for c in range(chunks):
        cut = slice(c * chunk, (c + 1) * chunk)
        for inner in range(per_owner):
            span = pl.ds(inner * step_rows, step_rows)
            first = owner * per_owner * step_rows + inner * step_rows
            summed = part[pl.ds(pl.multiple_of(first, step_rows), step_rows), cut]
            for offset in range(1, owners):
                source = lax.rem(owner + offset, owners)
                score_await(source, inner, c).wait_recv()
                summed = summed + arrived[source, span, cut]
            out_ref[span, cut] = summed

    def await_sent(step):
        source = neighbour(step)
        for offset in range(1, modules):
            block_copy(lax.rem(x + offset, modules), source).wait_send()
        if not (isinstance(step, int) and step == 0):
            block_copy(x, source).wait_send()

        @pl.when(source // per_owner != owner)
        def _():
            for c in range(chunks):
                score_copy(source, c).wait_send()

    await_sent(0)
    each(replays - 1, lambda index: await_sent(index + 1))


def pin(array):
    return pltpu.with_memory_space_constraint(array, pltpu.HBM)


def body(
    replays,
    modules,
    halves,
    new_factors,
    new_counts,
    new_ids,
    replay_grads,
    replay_ids,
    slot_module,
    output_inverse,
    input_inverse,
):
    examples, _, _, width = new_factors.shape
    feat = width // 2
    columns, _, depth = replay_grads.shape
    share = depth // feat
    total = replays * modules * examples
    owners = modules * halves
    rows = total // owners
    chunk = 384 if columns % 384 == 0 else columns // LATE
    hbm = pl.BlockSpec(memory_space=pltpu.HBM)
    smem = pl.BlockSpec(memory_space=pltpu.SMEM)
    summed = pl.pallas_call(
        functools.partial(kernel, (replays, modules, halves, chunk)),
        out_shape=jax.ShapeDtypeStruct((rows, columns), jnp.float32),
        in_specs=[smem, smem, hbm, hbm, hbm, hbm],
        out_specs=pl.BlockSpec(memory_space=pltpu.VMEM),
        scratch_shapes=[
            pltpu.VMEM(new_factors.shape, jnp.bfloat16),
            pltpu.VMEM((columns, depth), jnp.bfloat16),
            pltpu.VMEM(output_inverse.shape, jnp.float32),
            pltpu.VMEM(input_inverse.shape, jnp.float32),
            pltpu.VMEM((examples * share, 2 * feat), jnp.float32),
            pltpu.VMEM((modules, examples, depth), jnp.bfloat16),
            pltpu.VMEM((replays * modules, examples, depth), jnp.bfloat16),
            pltpu.VMEM((total, columns), jnp.float32),
            pltpu.VMEM((owners, rows, columns), jnp.float32),
            pltpu.SemaphoreType.DMA((4,)),
            pltpu.SemaphoreType.DMA((replays * modules,)),
            pltpu.SemaphoreType.DMA((replays * modules,)),
            pltpu.SemaphoreType.DMA((replays, columns // chunk)),
            pltpu.SemaphoreType.DMA((owners, replays // owners, columns // chunk)),
        ],
        compiler_params=pltpu.CompilerParams(
            collective_id=0, has_side_effects=True, vmem_limit_bytes=24 * 1024 * 1024
        ),
        name="attribution",
    )(
        slot_module,
        new_counts,
        pin(new_factors),
        pin(replay_grads.reshape(columns, depth)),
        pin(output_inverse),
        pin(input_inverse),
    )
    self_pairs = new_ids[:, None] == replay_ids[None, :]
    return jnp.where(self_pairs, jnp.zeros((), jnp.float32), summed)


def solution(mesh):
    in_specs = (
        P(("groups", "replay", "module"), None, None, None),
        P(("groups", "replay", "module")),
        P(("groups", "module", "half")),
        P(("groups", "replay"), "module", "half"),
        P(("groups", "replay")),
        P(),
        P(),
        P(),
    )
    out_specs = P(("groups", "module", "half"), "replay")
    return jax.shard_map(
        functools.partial(body, mesh.shape["replay"], mesh.shape["module"], mesh.shape["half"]),
        mesh=mesh,
        in_specs=in_specs,
        out_specs=out_specs,
        check_vma=False,
    )
```

```python
import functools

import jax
import jax.numpy as jnp
from jax import lax
from jax.experimental import pallas as pl
from jax.experimental.pallas import tpu as pltpu
from jax.sharding import PartitionSpec as P

MESH = pl.DeviceIdType.MESH
UNROLL = 16
EARLY = 1
LATE = 2


def each(count, step):
    if count <= UNROLL:
        for index in range(count):
            step(index)
    else:
        def one(index, carry):
            step(index)
            return carry

        lax.fori_loop(0, count, one, 0)


def parts_of(value):
    high = value.astype(jnp.bfloat16)
    low = (value - high.astype(jnp.float32)).astype(jnp.bfloat16)
    return high, low


def kernel(
    sizes,
    slot_module_hbm,
    counts_hbm,
    factors_hbm,
    replay_hbm,
    left_hbm,
    right_hbm,
    out_ref,
    slot_module,
    counts,
    factors,
    replay,
    left,
    right,
    rows_f32,
    outgoing,
    blocks,
    part,
    arrived,
    load_sem,
    send_sem,
    recv_sem,
    score_send_sem,
    score_recv_sem,
):
    replays, modules, halves, chunk = sizes
    z, x, h = lax.axis_index("replay"), lax.axis_index("module"), lax.axis_index("half")
    block = z * modules + x
    owner = x * halves + h
    owners = modules * halves
    examples, _, tokens, width = factors.shape
    feat = width // 2
    share = replay.shape[1] // feat
    columns = replay.shape[0]
    chunks = columns // chunk

    barrier = pltpu.get_barrier_semaphore()

    def greet_block(offset):
        target = lax.rem(block + offset + 1, replays * modules)
        pl.semaphore_signal(
            barrier,
            inc=1,
            device_id={"replay": target // modules, "module": lax.rem(target, modules)},
            device_id_type=MESH,
        )

    def greet_owner(offset):
        index = lax.rem(h + offset % (halves - 1) + 1, halves)
        pl.semaphore_signal(
            barrier,
            inc=1,
            device_id={"module": offset // (halves - 1), "half": index},
            device_id_type=MESH,
        )

    each(replays * modules - 1, greet_block)
    for offset in range(modules * (halves - 1)):
        greet_owner(offset)

    small_loads = [
        pltpu.make_async_copy(factors_hbm, factors, load_sem.at[0]),
        pltpu.make_async_copy(left_hbm, left, load_sem.at[1]),
        pltpu.make_async_copy(right_hbm, right, load_sem.at[2]),
        pltpu.make_async_copy(slot_module_hbm, slot_module, load_sem.at[4]),
        pltpu.make_async_copy(counts_hbm, counts, load_sem.at[5]),
    ]
    for load in small_loads:
        load.start()
    replay_load = pltpu.make_async_copy(replay_hbm, replay, load_sem.at[3])
    replay_load.start()

    for load in small_loads:
        load.wait()

    pair = 128 // tokens
    lane = lax.broadcasted_iota(jnp.int32, (share, 128), 1)
    zero = jnp.zeros((), jnp.bfloat16)
    low_lanes = lax.broadcasted_iota(jnp.int32, (examples, 2 * feat), 1) < feat

    def precondition(slot):
        module = slot_module[slot]
        entries = factors[:, module].reshape(examples * tokens, width)
        doubled = jnp.concatenate([entries, entries], axis=1)
        right_high, right_low = parts_of(right[module])
        blank = jnp.zeros((feat, feat), jnp.bfloat16)
        right_rows = jnp.concatenate([right_high, blank, right_low, blank], axis=0)
        right_rows = jnp.concatenate([right_rows, right_rows], axis=1)
        v = jnp.dot(doubled, right_rows, preferred_element_type=jnp.float32)
        left_high, left_low = parts_of(left[module, pl.ds(pl.multiple_of(h * share, share), share), :])
        left_blank = jnp.zeros((share, feat), jnp.bfloat16)
        left_columns = jnp.concatenate([left_blank, left_high, left_blank, left_low], axis=1)
        u = lax.dot_general(
            left_columns, doubled, (((1,), (1,)), ((), ())), preferred_element_type=jnp.float32
        )
        v_high, v_low = parts_of(v)
        for group in range(examples // pair):
            u_pair = u[:, group * 128 : (group + 1) * 128]
            masked = []
            for inner in range(pair):
                count = counts[group * pair + inner]
                first = inner * tokens
                keep = (lane >= first) & (lane < first + count)
                masked.append(jnp.where(keep, u_pair, 0.0))
            u_high, u_low = parts_of(jnp.concatenate(masked, axis=0))
            lhs = jnp.concatenate([u_high, u_high, u_low], axis=1)
            span = slice(group * 128, (group + 1) * 128)
            rhs = jnp.concatenate([v_high[span], v_low[span], v_high[span]], axis=0)
            rows_f32[pl.ds(group * pair * share, pair * share), :] = jnp.dot(
                lhs, rhs, preferred_element_type=jnp.float32
            )
        for q in range(share // 2):
            even = rows_f32[pl.ds(2 * q, examples, stride=share), :]
            odd = rows_f32[pl.ds(2 * q + 1, examples, stride=share), :]
            outgoing[slot, :, q * 2 * feat : (q + 1) * 2 * feat] = jnp.where(low_lanes, even, odd).astype(
                jnp.bfloat16
            )

    def block_copy(slot, target_z):
        target = target_z * modules + slot
        return pltpu.make_async_remote_copy(
            src_ref=outgoing.at[slot],
            dst_ref=blocks.at[block],
            send_sem=send_sem.at[target],
            recv_sem=recv_sem.at[block],
            device_id={"replay": target_z, "module": slot},
            device_id_type=MESH,
        )

    for slot in range(modules):
        precondition(slot)
    blocks[block] = outgoing[x]
    pl.semaphore_wait(barrier, replays * modules - 1 + modules * (halves - 1))

    def neighbour(step):
        if replays & (replays - 1):
            return lax.rem(z + step, replays)
        other, bit = z, 1
        while bit < replays:
            other = other + bit * ((step // bit) % 2) * (1 - 2 * ((z // bit) % 2))
            bit *= 2
        return other

    def send_blocks(step):
        for offset in range(1, modules):
            block_copy(lax.rem(x + offset, modules), neighbour(step)).start()
        if not (isinstance(step, int) and step == 0):
            block_copy(x, neighbour(step)).start()

    send_blocks(0)
    each(replays - 1, lambda index: send_blocks(1 + (index + 1) % (replays - 1)))

    per_owner = replays // owners
    step_rows = modules * examples

    def await_block(slot, source):
        pltpu.make_async_remote_copy(
            src_ref=outgoing.at[0],
            dst_ref=blocks.at[source],
            send_sem=send_sem.at[source],
            recv_sem=recv_sem.at[source],
            device_id={"replay": source // modules, "module": slot},
            device_id_type=MESH,
        ).wait_recv()

    def score_copy(source, c):
        cut = pl.ds(c * chunk, chunk)
        target = source // per_owner
        return pltpu.make_async_remote_copy(
            src_ref=part.at[pl.ds(pl.multiple_of(source * step_rows, step_rows), step_rows), cut],
            dst_ref=arrived.at[
                owner, pl.ds(pl.multiple_of((source % per_owner) * step_rows, step_rows), step_rows), cut
            ],
            send_sem=score_send_sem.at[source, c],
            recv_sem=score_recv_sem.at[owner, source % per_owner, c],
            device_id={"module": target // halves, "half": target % halves},
            device_id_type=MESH,
        )

    def score_await(source, inner, c):
        cut = pl.ds(c * chunk, chunk)
        return pltpu.make_async_remote_copy(
            src_ref=part.at[pl.ds(0, step_rows), cut],
            dst_ref=arrived.at[source, pl.ds(inner * step_rows, step_rows), cut],
            send_sem=score_send_sem.at[0, c],
            recv_sem=score_recv_sem.at[source, inner, c],
            device_id={"module": source // halves, "half": source % halves},
            device_id_type=MESH,
        )

    replay_load.wait()

    def await_step(step):
        source = neighbour(step)
        for offset in range(1, modules):
            slot = lax.rem(x + offset, modules)
            await_block(slot, source * modules + slot)
        if not (isinstance(step, int) and step == 0):
            await_block(x, source * modules + x)

    def score_steps(first, count, pieces):
        sources = [neighbour(first + inner) for inner in range(count)]
        lhs = jnp.concatenate(
            [blocks[source * modules + slot] for source in sources for slot in range(modules)], axis=0
        )
        for piece in range(pieces):
            span = columns // pieces
            cut = slice(piece * span, (piece + 1) * span)
            scores = lax.dot_general(
                lhs, replay[cut, :], (((1,), (1,)), ((), ())), preferred_element_type=jnp.float32
            )
            for inner, source in enumerate(sources):
                part[pl.ds(pl.multiple_of(source * step_rows, step_rows), step_rows), cut] = scores[
                    inner * step_rows : (inner + 1) * step_rows
                ]
            for source in sources:

                @pl.when(source // per_owner != owner)
                def _():
                    for c in range(piece * span // chunk, (piece + 1) * span // chunk):
                        score_copy(source, c).start()

    batch = 2 if replays % 2 == 0 else 1
    for inner in range(batch):
        await_step(inner)
    score_steps(0, batch, EARLY)

    def later(index):
        for inner in range(batch):
            await_step((index + 1) * batch + inner)
        score_steps((index + 1) * batch, batch, LATE)

    each(replays // batch - 1, later)

    for c in range(chunks):
        cut = slice(c * chunk, (c + 1) * chunk)
        for inner in range(per_owner):
            span = pl.ds(inner * step_rows, step_rows)
            first = owner * per_owner * step_rows + inner * step_rows
            summed = part[pl.ds(pl.multiple_of(first, step_rows), step_rows), cut]
            for offset in range(1, owners):
                source = lax.rem(owner + offset, owners)
                score_await(source, inner, c).wait_recv()
                summed = summed + arrived[source, span, cut]
            out_ref[span, cut] = summed

    def await_sent(step):
        source = neighbour(step)
        for offset in range(1, modules):
            block_copy(lax.rem(x + offset, modules), source).wait_send()
        if not (isinstance(step, int) and step == 0):
            block_copy(x, source).wait_send()

        @pl.when(source // per_owner != owner)
        def _():
            for c in range(chunks):
                score_copy(source, c).wait_send()

    await_sent(0)
    each(replays - 1, lambda index: await_sent(index + 1))


def pin(array):
    return pltpu.with_memory_space_constraint(array, pltpu.HBM)


def body(
    replays,
    modules,
    halves,
    new_factors,
    new_counts,
    new_ids,
    replay_grads,
    replay_ids,
    slot_module,
    output_inverse,
    input_inverse,
):
    examples, _, _, width = new_factors.shape
    feat = width // 2
    columns, _, depth = replay_grads.shape
    share = depth // feat
    total = replays * modules * examples
    owners = modules * halves
    rows = total // owners
    chunk = 384 if columns % 384 == 0 else columns // LATE
    hbm = pl.BlockSpec(memory_space=pltpu.HBM)
    summed = pl.pallas_call(
        functools.partial(kernel, (replays, modules, halves, chunk)),
        out_shape=jax.ShapeDtypeStruct((rows, columns), jnp.float32),
        in_specs=[hbm] * 6,
        out_specs=pl.BlockSpec(memory_space=pltpu.VMEM),
        scratch_shapes=[
            pltpu.SMEM(slot_module.shape, jnp.int32),
            pltpu.SMEM(new_counts.shape, jnp.int32),
            pltpu.VMEM(new_factors.shape, jnp.bfloat16),
            pltpu.VMEM((columns, depth), jnp.bfloat16),
            pltpu.VMEM(output_inverse.shape, jnp.float32),
            pltpu.VMEM(input_inverse.shape, jnp.float32),
            pltpu.VMEM((examples * share, 2 * feat), jnp.float32),
            pltpu.VMEM((modules, examples, depth), jnp.bfloat16),
            pltpu.VMEM((replays * modules, examples, depth), jnp.bfloat16),
            pltpu.VMEM((total, columns), jnp.float32),
            pltpu.VMEM((owners, rows, columns), jnp.float32),
            pltpu.SemaphoreType.DMA((6,)),
            pltpu.SemaphoreType.DMA((replays * modules,)),
            pltpu.SemaphoreType.DMA((replays * modules,)),
            pltpu.SemaphoreType.DMA((replays, columns // chunk)),
            pltpu.SemaphoreType.DMA((owners, replays // owners, columns // chunk)),
        ],
        compiler_params=pltpu.CompilerParams(
            collective_id=0, has_side_effects=True, vmem_limit_bytes=24 * 1024 * 1024
        ),
        name="attribution",
    )(
        pin(slot_module),
        pin(new_counts),
        pin(new_factors),
        pin(replay_grads.reshape(columns, depth)),
        pin(output_inverse),
        pin(input_inverse),
    )
    self_pairs = new_ids[:, None] == replay_ids[None, :]
    return jnp.where(self_pairs, jnp.zeros((), jnp.float32), summed)


def solution(mesh):
    in_specs = (
        P(("groups", "replay", "module"), None, None, None),
        P(("groups", "replay", "module")),
        P(("groups", "module", "half")),
        P(("groups", "replay"), "module", "half"),
        P(("groups", "replay")),
        P(),
        P(),
        P(),
    )
    out_specs = P(("groups", "module", "half"), "replay")
    return jax.shard_map(
        functools.partial(body, mesh.shape["replay"], mesh.shape["module"], mesh.shape["half"]),
        mesh=mesh,
        in_specs=in_specs,
        out_specs=out_specs,
        check_vma=False,
    )
```

```python
import functools

import jax
import jax.numpy as jnp
from jax import lax
from jax.experimental import pallas as pl
from jax.experimental.pallas import tpu as pltpu
from jax.sharding import PartitionSpec as P

MESH = pl.DeviceIdType.MESH
UNROLL = 16
EARLY = 1
LATE = 2


def each(count, step):
    if count <= UNROLL:
        for index in range(count):
            step(index)
    else:
        def one(index, carry):
            step(index)
            return carry

        lax.fori_loop(0, count, one, 0)


def parts_of(value):
    high = value.astype(jnp.bfloat16)
    low = (value - high.astype(jnp.float32)).astype(jnp.bfloat16)
    return high, low


def kernel(
    sizes,
    slot_module_hbm,
    counts_hbm,
    factors_hbm,
    replay_hbm,
    left_hbm,
    right_hbm,
    out_ref,
    slot_module,
    counts,
    factors,
    replay,
    left,
    right,
    rows_f32,
    outgoing,
    blocks,
    part,
    arrived,
    load_sem,
    send_sem,
    recv_sem,
    score_send_sem,
    score_recv_sem,
):
    replays, modules, halves, chunk = sizes
    z, x, h = lax.axis_index("replay"), lax.axis_index("module"), lax.axis_index("half")
    block = z * modules + x
    owner = x * halves + h
    owners = modules * halves
    examples, _, tokens, width = factors.shape
    feat = width // 2
    share = replay.shape[1] // feat
    columns = replay.shape[0]
    chunks = columns // chunk

    barrier = pltpu.get_barrier_semaphore()

    def greet_block(offset):
        target = lax.rem(block + offset + 1, replays * modules)
        pl.semaphore_signal(
            barrier,
            inc=1,
            device_id={"replay": target // modules, "module": lax.rem(target, modules)},
            device_id_type=MESH,
        )

    def greet_owner(offset):
        index = lax.rem(h + offset % (halves - 1) + 1, halves)
        pl.semaphore_signal(
            barrier,
            inc=1,
            device_id={"module": offset // (halves - 1), "half": index},
            device_id_type=MESH,
        )

    each(replays * modules - 1, greet_block)
    for offset in range(modules * (halves - 1)):
        greet_owner(offset)

    small_loads = [
        pltpu.make_async_copy(factors_hbm, factors, load_sem.at[0]),
        pltpu.make_async_copy(left_hbm, left, load_sem.at[1]),
        pltpu.make_async_copy(right_hbm, right, load_sem.at[2]),
        pltpu.make_async_copy(slot_module_hbm, slot_module, load_sem.at[4]),
        pltpu.make_async_copy(counts_hbm, counts, load_sem.at[5]),
    ]
    for load in small_loads:
        load.start()
    replay_load = pltpu.make_async_copy(replay_hbm, replay, load_sem.at[3])

    for load in small_loads:
        load.wait()

    pair = 128 // tokens
    lane = lax.broadcasted_iota(jnp.int32, (share, 128), 1)
    zero = jnp.zeros((), jnp.bfloat16)
    low_lanes = lax.broadcasted_iota(jnp.int32, (examples, 2 * feat), 1) < feat

    def precondition(slot):
        module = slot_module[slot]
        entries = factors[:, module].reshape(examples * tokens, width)
        doubled = jnp.concatenate([entries, entries], axis=1)
        right_high, right_low = parts_of(right[module])
        blank = jnp.zeros((feat, feat), jnp.bfloat16)
        right_rows = jnp.concatenate([right_high, blank, right_low, blank], axis=0)
        right_rows = jnp.concatenate([right_rows, right_rows], axis=1)
        v = jnp.dot(doubled, right_rows, preferred_element_type=jnp.float32)
        left_high, left_low = parts_of(left[module, pl.ds(pl.multiple_of(h * share, share), share), :])
        left_blank = jnp.zeros((share, feat), jnp.bfloat16)
        left_columns = jnp.concatenate([left_blank, left_high, left_blank, left_low], axis=1)
        u = lax.dot_general(
            left_columns, doubled, (((1,), (1,)), ((), ())), preferred_element_type=jnp.float32
        )
        v_high, v_low = parts_of(v)
        for group in range(examples // pair):
            u_pair = u[:, group * 128 : (group + 1) * 128]
            masked = []
            for inner in range(pair):
                count = counts[group * pair + inner]
                first = inner * tokens
                keep = (lane >= first) & (lane < first + count)
                masked.append(jnp.where(keep, u_pair, 0.0))
            u_high, u_low = parts_of(jnp.concatenate(masked, axis=0))
            lhs = jnp.concatenate([u_high, u_high, u_low], axis=1)
            span = slice(group * 128, (group + 1) * 128)
            rhs = jnp.concatenate([v_high[span], v_low[span], v_high[span]], axis=0)
            rows_f32[pl.ds(group * pair * share, pair * share), :] = jnp.dot(
                lhs, rhs, preferred_element_type=jnp.float32
            )
        for q in range(share // 2):
            even = rows_f32[pl.ds(2 * q, examples, stride=share), :]
            odd = rows_f32[pl.ds(2 * q + 1, examples, stride=share), :]
            outgoing[slot, :, q * 2 * feat : (q + 1) * 2 * feat] = jnp.where(low_lanes, even, odd).astype(
                jnp.bfloat16
            )

    def block_copy(slot, target_z):
        target = target_z * modules + slot
        return pltpu.make_async_remote_copy(
            src_ref=outgoing.at[slot],
            dst_ref=blocks.at[block],
            send_sem=send_sem.at[target],
            recv_sem=recv_sem.at[block],
            device_id={"replay": target_z, "module": slot},
            device_id_type=MESH,
        )

    replay_load.start()
    for slot in range(modules):
        precondition(slot)
    blocks[block] = outgoing[x]
    pl.semaphore_wait(barrier, replays * modules - 1 + modules * (halves - 1))

    def neighbour(step):
        if replays & (replays - 1):
            return lax.rem(z + step, replays)
        other, bit = z, 1
        while bit < replays:
            other = other + bit * ((step // bit) % 2) * (1 - 2 * ((z // bit) % 2))
            bit *= 2
        return other

    def send_blocks(step):
        for offset in range(1, modules):
            block_copy(lax.rem(x + offset, modules), neighbour(step)).start()
        if not (isinstance(step, int) and step == 0):
            block_copy(x, neighbour(step)).start()

    each(replays - 1, lambda index: send_blocks(1 + (index + 1) % (replays - 1)))

    send_blocks(0)

    per_owner = replays // owners
    step_rows = modules * examples

    def await_block(slot, source):
        pltpu.make_async_remote_copy(
            src_ref=outgoing.at[0],
            dst_ref=blocks.at[source],
            send_sem=send_sem.at[source],
            recv_sem=recv_sem.at[source],
            device_id={"replay": source // modules, "module": slot},
            device_id_type=MESH,
        ).wait_recv()

    def score_copy(source, c):
        cut = pl.ds(c * chunk, chunk)
        target = source // per_owner
        return pltpu.make_async_remote_copy(
            src_ref=part.at[pl.ds(pl.multiple_of(source * step_rows, step_rows), step_rows), cut],
            dst_ref=arrived.at[
                owner, pl.ds(pl.multiple_of((source % per_owner) * step_rows, step_rows), step_rows), cut
            ],
            send_sem=score_send_sem.at[source, c],
            recv_sem=score_recv_sem.at[owner, source % per_owner, c],
            device_id={"module": target // halves, "half": target % halves},
            device_id_type=MESH,
        )

    def score_await(source, inner, c):
        cut = pl.ds(c * chunk, chunk)
        return pltpu.make_async_remote_copy(
            src_ref=part.at[pl.ds(0, step_rows), cut],
            dst_ref=arrived.at[source, pl.ds(inner * step_rows, step_rows), cut],
            send_sem=score_send_sem.at[0, c],
            recv_sem=score_recv_sem.at[source, inner, c],
            device_id={"module": source // halves, "half": source % halves},
            device_id_type=MESH,
        )

    replay_load.wait()

    def await_step(step):
        source = neighbour(step)
        for offset in range(1, modules):
            slot = lax.rem(x + offset, modules)
            await_block(slot, source * modules + slot)
        if not (isinstance(step, int) and step == 0):
            await_block(x, source * modules + x)

    def score_steps(first, count, pieces):
        sources = [neighbour(first + inner) for inner in range(count)]
        lhs = jnp.concatenate(
            [blocks[source * modules + slot] for source in sources for slot in range(modules)], axis=0
        )
        for piece in range(pieces):
            span = columns // pieces
            cut = slice(piece * span, (piece + 1) * span)
            scores = lax.dot_general(
                lhs, replay[cut, :], (((1,), (1,)), ((), ())), preferred_element_type=jnp.float32
            )
            for inner, source in enumerate(sources):
                part[pl.ds(pl.multiple_of(source * step_rows, step_rows), step_rows), cut] = scores[
                    inner * step_rows : (inner + 1) * step_rows
                ]
            for source in sources:

                @pl.when(source // per_owner != owner)
                def _():
                    for c in range(piece * span // chunk, (piece + 1) * span // chunk):
                        score_copy(source, c).start()

    batch = 2 if replays % 2 == 0 else 1
    for inner in range(batch):
        await_step(inner)
    score_steps(0, batch, EARLY)

    def later(index):
        for inner in range(batch):
            await_step((index + 1) * batch + inner)
        score_steps((index + 1) * batch, batch, LATE)

    each(replays // batch - 1, later)

    for c in range(chunks):
        cut = slice(c * chunk, (c + 1) * chunk)
        for inner in range(per_owner):
            span = pl.ds(inner * step_rows, step_rows)
            first = owner * per_owner * step_rows + inner * step_rows
            summed = part[pl.ds(pl.multiple_of(first, step_rows), step_rows), cut]
            for offset in range(1, owners):
                source = lax.rem(owner + offset, owners)
                score_await(source, inner, c).wait_recv()
                summed = summed + arrived[source, span, cut]
            out_ref[span, cut] = summed

    def await_sent(step):
        source = neighbour(step)
        for offset in range(1, modules):
            block_copy(lax.rem(x + offset, modules), source).wait_send()
        if not (isinstance(step, int) and step == 0):
            block_copy(x, source).wait_send()

        @pl.when(source // per_owner != owner)
        def _():
            for c in range(chunks):
                score_copy(source, c).wait_send()

    await_sent(0)
    each(replays - 1, lambda index: await_sent(index + 1))


def pin(array):
    return pltpu.with_memory_space_constraint(array, pltpu.HBM)


def body(
    replays,
    modules,
    halves,
    new_factors,
    new_counts,
    new_ids,
    replay_grads,
    replay_ids,
    slot_module,
    output_inverse,
    input_inverse,
):
    examples, _, _, width = new_factors.shape
    feat = width // 2
    columns, _, depth = replay_grads.shape
    share = depth // feat
    total = replays * modules * examples
    owners = modules * halves
    rows = total // owners
    chunk = 384 if columns % 384 == 0 else columns // LATE
    hbm = pl.BlockSpec(memory_space=pltpu.HBM)
    summed = pl.pallas_call(
        functools.partial(kernel, (replays, modules, halves, chunk)),
        out_shape=jax.ShapeDtypeStruct((rows, columns), jnp.float32),
        in_specs=[hbm] * 6,
        out_specs=pl.BlockSpec(memory_space=pltpu.VMEM),
        scratch_shapes=[
            pltpu.SMEM(slot_module.shape, jnp.int32),
            pltpu.SMEM(new_counts.shape, jnp.int32),
            pltpu.VMEM(new_factors.shape, jnp.bfloat16),
            pltpu.VMEM((columns, depth), jnp.bfloat16),
            pltpu.VMEM(output_inverse.shape, jnp.float32),
            pltpu.VMEM(input_inverse.shape, jnp.float32),
            pltpu.VMEM((examples * share, 2 * feat), jnp.float32),
            pltpu.VMEM((modules, examples, depth), jnp.bfloat16),
            pltpu.VMEM((replays * modules, examples, depth), jnp.bfloat16),
            pltpu.VMEM((total, columns), jnp.float32),
            pltpu.VMEM((owners, rows, columns), jnp.float32),
            pltpu.SemaphoreType.DMA((6,)),
            pltpu.SemaphoreType.DMA((replays * modules,)),
            pltpu.SemaphoreType.DMA((replays * modules,)),
            pltpu.SemaphoreType.DMA((replays, columns // chunk)),
            pltpu.SemaphoreType.DMA((owners, replays // owners, columns // chunk)),
        ],
        compiler_params=pltpu.CompilerParams(
            collective_id=0, has_side_effects=True, vmem_limit_bytes=24 * 1024 * 1024
        ),
        name="attribution",
    )(
        pin(slot_module),
        pin(new_counts),
        pin(new_factors),
        pin(replay_grads.reshape(columns, depth)),
        pin(output_inverse),
        pin(input_inverse),
    )
    self_pairs = new_ids[:, None] == replay_ids[None, :]
    return jnp.where(self_pairs, jnp.zeros((), jnp.float32), summed)


def solution(mesh):
    in_specs = (
        P(("groups", "replay", "module"), None, None, None),
        P(("groups", "replay", "module")),
        P(("groups", "module", "half")),
        P(("groups", "replay"), "module", "half"),
        P(("groups", "replay")),
        P(),
        P(),
        P(),
    )
    out_specs = P(("groups", "module", "half"), "replay")
    return jax.shard_map(
        functools.partial(body, mesh.shape["replay"], mesh.shape["module"], mesh.shape["half"]),
        mesh=mesh,
        in_specs=in_specs,
        out_specs=out_specs,
        check_vma=False,
    )
```
